32 devices in a mesh: groups: 2 (over x), ep: 16 (over z, y, core).
Axes of the slice: x: 2, y: 2, z: 4, core: 2. Of those that a mesh axis runs over, the one named last changes fastest.
Arguments:
- tokens: bfloat16 [2048, 2048], P(('groups', 'ep')), parts along dimension 0, may hold values from -6 to 6
- expert_ids: int32 [2048, 8], P(('groups', 'ep')), parts along dimension 0, may hold values from 0 to 15, as said below
- gate_values: float32 [2048, 8], P(('groups', 'ep')), parts along dimension 0, may hold values from 0.1 to 1
- expert_weights: bfloat16 [32, 2048, 3072], P(('groups', 'ep')), parts along dimension 0, as said below
- home_slot: int32 [32], P('groups'), parts along dimension 0, may hold values from 0 to 15, as said below
- spare_expert: int32 [32], P('groups'), parts along dimension 0, may hold values from -1 to 15, as said below
Outputs:
- moe_out: bfloat16 [2048, 2048], P(('groups', 'ep')), parts along dimension 0
The draws below stay inside these ranges and needn't reach their ends.
There are 2 independent parts, one for each index of `groups`. The reference program is written for one: setup_inputs(seed, part) draws one part's arguments, and reference() takes and returns one part's arrays. A program takes and returns all parts, laid end to end along the dimension named above; each array names one. Nothing has to cross between parts.
Inputs may be any that keep to these rules, and one draw needn't show every extreme that they name: `expert_ids`: each row names 8 different experts. `home_slot`: a permutation of the experts. `spare_expert`: each expert is named a multiple of 3 times, at most 6, and some expert exactly 3 * 2 times; -1 stands in as many entries as the remainder of 16 divided by 3. `expert_weights`: the second slot of the device holding the k-th third of a split copy of expert e equals the matching gate, up and down columns (hidden units k * 256 to (k + 1) * 256 - 1) of e's home block.
All inputs are finite; a program needn't handle non-finite values.
Results may differ from the reference program's by a relative error of at most 0.0058.
Values may be sent and summed in bfloat16 or wider, within the bound.
No kernel may reach another device: no remote copies, remote signals or barrier semaphores. Data moves between devices by JAX's collectives and lax.ppermute only.
A program may use at most 128 MiB of HBM per device.

```python
import jax
import jax.numpy as jnp
from jax import lax

D = 2048
FF = 768
TOP = 8
RMAX = 2
TOK_DEV = 64
EXPERTS = 16
TOKENS = 1024
CAP = 32
N_EP = 16


def placement(key):
    popular = jax.random.permutation(jax.random.fold_in(key, 7), EXPERTS).astype(jnp.int32)
    home = jax.random.permutation(jax.random.fold_in(key, 5), EXPERTS).astype(jnp.int32)
    copy_counts = jax.random.randint(jax.random.fold_in(key, 13), (EXPERTS,), 1, RMAX + 1, dtype=jnp.int32)
    copy_counts = copy_counts.at[0].set(RMAX)
    running = jnp.cumsum(copy_counts)
    positions = jnp.arange(EXPERTS, dtype=jnp.int32)
    copy_number = positions // 3
    hot_index = jnp.sum((running[None, :] <= copy_number[:, None]).astype(jnp.int32), axis=1)
    hot_index = jnp.minimum(hot_index, EXPERTS - 1).astype(jnp.int32)
    listed = jnp.where(positions < 3 * (EXPERTS // 3), popular[hot_index], -1).astype(jnp.int32)
    shuffled = jax.random.permutation(jax.random.fold_in(key, 17), EXPERTS).astype(jnp.int32)
    spare = jnp.zeros((EXPERTS,), jnp.int32).at[shuffled].set(listed)
    return (popular, home, spare.astype(jnp.int32))


def draw_home_slot(key, part):
    popular, home, spare = placement(key)
    return home


def draw_spare_expert(key, part):
    popular, home, spare = placement(key)
    return spare


def draw_expert_ids(key, part):
    popular, home, spare = placement(key)
    ranking = jnp.zeros((EXPERTS,), jnp.int32).at[popular].set(jnp.arange(EXPERTS, dtype=jnp.int32))
    lift_amount = 40 * jnp.maximum(0, 10 - ranking)
    scores = jax.random.randint(jax.random.fold_in(key, 11), (TOKENS, EXPERTS), 0, 1000, dtype=jnp.int32)
    scores = (scores + lift_amount[None, :]) * EXPERTS + jnp.arange(EXPERTS, dtype=jnp.int32)[None, :]
    return lax.top_k(scores, TOP)[1].astype(jnp.int32)


def draw_expert_weights(key, part):
    popular, home, spare = placement(key)
    width = 3 * FF
    third_width = FF // 3
    base = jax.random.truncated_normal(jax.random.fold_in(key, 23), -6.0, 6.0, (EXPERTS, D, width), jnp.float32)
    base = base * D ** (-0.5)
    device_range = jnp.arange(EXPERTS, dtype=jnp.int32)
    same_earlier = (spare[None, :] == spare[:, None]) & (device_range[None, :] < device_range[:, None])
    holder_rank = jnp.sum(same_earlier.astype(jnp.int32), axis=1)
    third_index = holder_rank % 3
    safe_expert = jnp.maximum(spare, 0)
    owner = jnp.sum(jnp.where(device_range[None, :] == safe_expert[:, None], home[None, :], 0), axis=1).astype(jnp.int32)
    within = jnp.arange(third_width, dtype=jnp.int32)
    start_col = third_index[:, None] * third_width + within[None, :]
    columns = jnp.concatenate([start_col, start_col + FF, start_col + 2 * FF], axis=1).astype(jnp.int32)
    row_range = jnp.arange(D, dtype=jnp.int32)
    copied = base[owner[:, None, None], row_range[None, :, None], columns[:, None, :]]
    return jnp.concatenate([base, copied], axis=2).astype(jnp.bfloat16)


def block_scale(key, extent, split, low, top_value):
    loudness, own = 1.0, jax.random.fold_in(key, 6)
    for dim, blocks in split:
        draws = jnp.exp(jax.random.uniform(jax.random.fold_in(own, dim), (blocks,), jnp.float32, low / len(split), top_value / len(split)))
        loudness = loudness * jnp.repeat(draws, extent[dim] // blocks).reshape([-1 if axis == dim else 1 for axis in range(len(extent))])
    return loudness


def noise(key, dims, scale, bound, cuts=(), held_as=jnp.bfloat16):
    result = scale * jax.random.normal(key, dims, jnp.float32)
    if cuts:
        result = result * block_scale(key, dims, cuts, -0.22, 0.18)
    return jnp.clip(result, -bound, bound).astype(held_as)


def setup_inputs(seed: int = 0, part: int = 0) -> dict:
    arg_keys = jax.random.split(jax.random.key(seed), 7)
    part_keys = jax.random.split(jax.random.fold_in(arg_keys[6], part), 7)
    return {
        "tokens": noise(part_keys[0], (TOKENS, D), 1.0, 6.0, ((0, 16),)),
        "expert_ids": draw_expert_ids(jax.random.fold_in(jax.random.fold_in(arg_keys[6], part), 71), part),
        "gate_values": jnp.clip(0.1 + 0.9 * jax.random.uniform(part_keys[2], (TOKENS, TOP), jnp.float32) ** block_scale(part_keys[2], (TOKENS, TOP), ((0, 16),), -0.2, 0.2), 0.1, 1.0),
        "expert_weights": draw_expert_weights(jax.random.fold_in(jax.random.fold_in(arg_keys[6], part), 71), part),
        "home_slot": draw_home_slot(jax.random.fold_in(jax.random.fold_in(arg_keys[6], part), 71), part),
        "spare_expert": draw_spare_expert(jax.random.fold_in(jax.random.fold_in(arg_keys[6], part), 71), part),
    }


def expert_rows(token_rows, weight_block):
    hidden_width = weight_block.shape[1] // 3
    gate_up = jnp.dot(token_rows, weight_block[:, :2 * hidden_width], preferred_element_type=jnp.float32)
    hidden = (jax.nn.silu(gate_up[:, :hidden_width]) * gate_up[:, hidden_width:]).astype(jnp.bfloat16)
    answer = lax.dot_general(hidden, weight_block[:, 2 * hidden_width:], (((1,), (1,)), ((), ())), preferred_element_type=jnp.float32)
    return answer.astype(jnp.bfloat16)


def host_tables(expert_ids, home_slot, spare_expert):
    devices = N_EP
    per_device = TOK_DEV * TOP
    ids_grid = expert_ids.reshape(devices, per_device).astype(jnp.int32)
    expert_range = jnp.arange(EXPERTS, dtype=jnp.int32)
    holders = (spare_expert[None, :] == expert_range[:, None]).astype(jnp.int32)
    copies = 1 + jnp.sum(holders, axis=1) // 3
    holder_rank = jnp.cumsum(holders, axis=1)
    chosen = (ids_grid[:, :, None] == expert_range[None, None, :]).astype(jnp.int32)
    earlier = jnp.cumsum(chosen, axis=1) - chosen
    arrival = jnp.sum(earlier * chosen, axis=2)
    copy_count = copies[ids_grid]
    copy_index = arrival % copy_count
    position = arrival // copy_count
    first_rank = 3 * copy_index - 2
    matched = (holders[ids_grid] == 1) & (holder_rank[ids_grid] == first_rank[:, :, None])
    device_range = jnp.arange(devices, dtype=jnp.int32)
    spare_device = jnp.sum(jnp.where(matched, device_range[None, None, :], 0), axis=2).astype(jnp.int32)
    host = jnp.where(copy_index == 0, 2 * home_slot[ids_grid], 2 * spare_device + 1)
    host = jnp.where(position < CAP, host, 2 * devices).astype(jnp.int32)
    column = (device_range[:, None] * CAP + position).astype(jnp.int32)
    assignment = jnp.arange(devices * per_device, dtype=jnp.int32).reshape(devices, per_device)
    table = jnp.full((2 * devices, devices * CAP), -1, dtype=jnp.int32)
    return table.at[host, column].set(assignment, mode="drop")


def reference(tokens, expert_ids, gate_values, expert_weights, home_slot, spare_expert):
    table = host_tables(expert_ids, home_slot, spare_expert)
    flat_gates = gate_values.reshape(-1)
    expert_range = jnp.arange(EXPERTS, dtype=jnp.int32)

    def one_host(total, host):
        device = (host // 2).astype(jnp.int32)
        spare_home = jnp.sum(jnp.where(expert_range == spare_expert[device], home_slot, 0)).astype(jnp.int32)
        block_index = jnp.where(host % 2 == 0, device, spare_home).astype(jnp.int32)
        weight_block = lax.dynamic_index_in_dim(expert_weights, block_index, 0, keepdims=False)[:, :3 * FF]
        entries = table[host]
        valid = entries >= 0
        safe_entries = jnp.where(valid, entries, 0).astype(jnp.int32)
        token_index = (safe_entries // TOP).astype(jnp.int32)
        answers = expert_rows(tokens[token_index], weight_block)
        scaling = jnp.where(valid, flat_gates[safe_entries], jnp.zeros_like(flat_gates[safe_entries]))
        total = total.at[token_index].add(answers.astype(jnp.float32) * scaling[:, None])
        return total, None

    start_total = jnp.zeros((TOKENS, D), dtype=jnp.float32)
    total, unused = lax.scan(one_host, start_total, jnp.arange(2 * N_EP, dtype=jnp.int32))
    return total.astype(jnp.bfloat16)
```

```python
import functools

import jax
import jax.numpy as jnp
from jax import lax
from jax.experimental import pallas as pl
from jax.experimental.pallas import tpu as pltpu
from jax.sharding import PartitionSpec as P

LANES = 128
SUBS = 16
THIRD = 3
VMEM = pl.BlockSpec(memory_space=pltpu.VMEM)
SMEM = pl.BlockSpec(memory_space=pltpu.SMEM)


class Packing:
    def __init__(self, local_tokens, feature, experts):
        self.local_tokens = local_tokens
        self.feature = feature
        self.experts = experts
        self.cols = feature // LANES
        self.groups = local_tokens // SUBS
        self.half = self.groups // 2
        self.per_tile = max(1, LANES // (2 * experts))
        self.gate_tiles = pl.cdiv(self.groups, self.per_tile)
        self.tiles = self.groups * self.cols + self.gate_tiles
        self.split = self.half * self.cols

    def tile(self, group):
        return group * self.cols + (self.gate_tiles if group >= self.half else 0)


def pack_body(pk, capacity, devices, tokens_ref, ids_ref, gates_ref, spare_ref, out_ref):
    for group in range(pk.groups):
        for col in range(pk.cols):
            out_ref[pk.tile(group) + col] = tokens_ref[
                group * SUBS : (group + 1) * SUBS, col * LANES : (col + 1) * LANES
            ]
    rows = pk.local_tokens
    lane = lax.broadcasted_iota(jnp.int32, (1, LANES), 1)
    expert = lax.rem(lane, pk.experts)
    chosen = jnp.zeros((rows, LANES), jnp.float32)
    gate = jnp.zeros((rows, LANES), jnp.float32)
    for k in range(ids_ref.shape[1]):
        match = ids_ref[:, k : k + 1] == expert
        chosen = jnp.where(match, 1.0, chosen)
        gate = jnp.where(match, gates_ref[:, k : k + 1], gate)
    before = (
        lax.broadcasted_iota(jnp.int32, (rows, rows), 0)
        > lax.broadcasted_iota(jnp.int32, (rows, rows), 1)
    ).astype(jnp.float32).astype(jnp.bfloat16)
    arrival = jnp.dot(before, chosen.astype(jnp.bfloat16), preferred_element_type=jnp.float32)
    named = jnp.zeros((1, LANES), jnp.int32)
    for device in range(devices):
        named = named + (expert == spare_ref[device]).astype(jnp.int32)
    count = jnp.ones((1, LANES), jnp.int32)
    for copy in range(1, devices // THIRD + 1):
        count = count + (named >= THIRD * copy).astype(jnp.int32)
    gate = jnp.where(arrival < (count * capacity).astype(jnp.float32), gate, 0.0)
    high = gate.astype(jnp.bfloat16).astype(jnp.float32)
    low = gate - high
    value = jnp.where(lax.rem(lane // pk.experts, 2) == 0, high, low)
    slot = lane // (2 * pk.experts)
    for index in range(pk.gate_tiles):
        tile = jnp.zeros((SUBS, LANES), jnp.float32)
        for part in range(pk.per_tile):
            group = index * pk.per_tile + part
            if group < pk.groups:
                tile = jnp.where(slot == part, value[group * SUBS : (group + 1) * SUBS], tile)
        out_ref[pk.split + index] = tile.astype(jnp.bfloat16)


def pack(pk, capacity, devices, tokens, ids, gates, spare):
    return pl.pallas_call(
        functools.partial(pack_body, pk, capacity, devices),
        out_shape=jax.ShapeDtypeStruct((pk.tiles, SUBS, LANES), jnp.bfloat16),
        in_specs=[VMEM, VMEM, VMEM, SMEM],
        out_specs=VMEM,
        name="pack",
    )(tokens, ids, gates, spare)


def chunk_body(pk, pieces, outs, steps, *refs):
    count = len(pieces)
    home_ref, me_ref = refs[:2]
    buffers = refs[2 : 2 + count]
    gate_w, up_w, down_w = refs[2 + count : 5 + count]
    out_refs = refs[5 + count : 5 + count + len(outs)]
    x_ref, acc_ref = refs[5 + count + len(outs) :]
    step = pl.program_id(0)

    @pl.when(step == 0)
    def _():
        row = 0
        for buffer, groups in zip(buffers, pieces):
            for first, _, _ in groups:
                for col in range(pk.cols):
                    x_ref[row : row + SUBS, col * LANES : (col + 1) * LANES] = buffer[first + col]
                row += SUBS

    rows = x_ref[...]
    gate = jnp.dot(rows, gate_w[0], preferred_element_type=jnp.float32)
    up = jnp.dot(rows, up_w[0], preferred_element_type=jnp.float32)
    hidden = (gate / (1.0 + jnp.exp(-gate)) * up).astype(jnp.bfloat16)
    part = lax.dot_general(
        hidden, down_w[0], (((1,), (1,)), ((), ())), preferred_element_type=jnp.float32
    )

    @pl.when(step == 0)
    def _():
        acc_ref[...] = part

    @pl.when(step > 0)
    def _():
        acc_ref[...] += part

    @pl.when(step == steps - 1)
    def _():
        mine = jnp.int32(0)
        for e in range(pk.experts):
            mine = jnp.where(home_ref[e] == me_ref[0], e, mine)
        lane = lax.broadcasted_iota(jnp.int32, (1, LANES), 1)
        scales = []
        for buffer, groups in zip(buffers, pieces):
            for _, gate_tile, slot in groups:
                place = slot * 2 * pk.experts + mine
                wanted = (lane == place) | (lane == place + pk.experts)
                table = buffer[gate_tile].astype(jnp.float32)
                scales.append(jnp.sum(jnp.where(wanted, table, 0.0), axis=1, keepdims=True))
        row = 0
        for out_ref in out_refs:
            for start in range(0, out_ref.shape[0], SUBS):
                scaled = acc_ref[row : row + SUBS, :] * scales[row // SUBS]
                out_ref[start : start + SUBS, :] = scaled.astype(out_ref.dtype)
                row += SUBS


def chunk(pk, weights, home, me, own, crossed, outs):
    hidden_width = weights.shape[2] // 4
    block = hidden_width // THIRD
    steps = hidden_width // block
    pieces = []
    for buffer, kind in own + crossed:
        if kind == "first":
            picked, shift = range(pk.half), 0
        elif kind == "second":
            picked, shift = range(pk.half, pk.groups), pk.split
        else:
            picked, shift = range(pk.groups), 0
        pieces.append(
            [
                (
                    pk.tile(g) - shift,
                    pk.split - shift + g // pk.per_tile,
                    g % pk.per_tile,
                )
                for g in picked
            ]
        )
    buffers = [buffer for buffer, _ in own + crossed]
    total = SUBS * sum(len(groups) for groups in pieces)
    width = pk.feature

    def weight_spec(offset):
        return pl.BlockSpec((1, width, block), lambda j: (0, 0, offset * steps + j))

    flops = 2 * total * width * 3 * hidden_width
    moved = 2 * width * 3 * hidden_width + 4 * total * width
    return pl.pallas_call(
        functools.partial(chunk_body, pk, pieces, outs, steps),
        grid=(steps,),
        out_shape=[jax.ShapeDtypeStruct((r, width), d) for r, d in outs],
        in_specs=[SMEM, SMEM]
        + [pl.BlockSpec(b.shape, lambda j: (0, 0, 0)) for b in buffers]
        + [weight_spec(0), weight_spec(1), weight_spec(2)],
        out_specs=[pl.BlockSpec((r, width), lambda j: (0, 0)) for r, _ in outs],
        scratch_shapes=[
            pltpu.VMEM((total, width), jnp.bfloat16),
            pltpu.VMEM((total, width), jnp.float32),
        ],
        compiler_params=pltpu.CompilerParams(dimension_semantics=("arbitrary",)),
        cost_estimate=pl.CostEstimate(
            flops=flops, transcendentals=total * hidden_width, bytes_accessed=moved
        ),
        name="chunk",
    )(home, me, *buffers, weights, weights, weights)


def shards(tokens, expert_ids, gate_values, expert_weights, home_slot, spare_expert):
    devices = lax.axis_size("ep")
    local_tokens, feature = tokens.shape
    capacity = local_tokens * expert_ids.shape[1] // devices
    pk = Packing(local_tokens, feature, home_slot.shape[0])
    chips = devices // 2
    far = chips // 2
    ring = list(range(0, chips, 2)) + list(range(chips - 1, 0, -2))
    ahead = [
        (2 * ring[i] + c, 2 * ring[(i + 1) % chips] + c) for i in range(chips) for c in range(2)
    ]
    back = [(t, s) for s, t in ahead]
    pair = [(d, d ^ 1) for d in range(devices)]
    wire = jnp.bfloat16 if chips <= 8 else jnp.float32

    def send(x, where):
        return lax.ppermute(x, "ep", where)

    me = lax.axis_index("ep").astype(jnp.int32).reshape(1)
    run = functools.partial(chunk, pk, expert_weights, home_slot, me)
    packed = pack(pk, capacity, devices, tokens, expert_ids, gate_values, spare_expert)

    half_rows = pk.half * SUBS
    keep, give = {}, {}
    f = b = packed
    keep_own, give_own = run(
        [(packed, "all")],
        [(send(packed, pair), "all")],
        [(local_tokens, jnp.float32), (local_tokens, jnp.bfloat16)],
    )
    for r in range(1, far):
        f, b = send(f, ahead), send(b, back)
        fx, bx = send(f, pair), send(b, pair)
        keep_f, keep_b, gave = run(
            [(f, "all"), (b, "all")],
            [(fx, "all"), (bx, "all")],
            [
                (local_tokens, jnp.float32),
                (local_tokens, jnp.float32),
                (2 * local_tokens, jnp.bfloat16),
            ],
        )
        keep[r] = (keep_f, keep_b)
        give[r] = send(gave, pair)
    give_own = send(give_own, pair)
    cut = pk.split + pk.gate_tiles
    f, b = send(f[:cut], ahead), send(b[pk.split :], back)
    fx, bx = send(f, pair), send(b, pair)
    keep_far, gave = run(
        [(f, "first"), (b, "second")],
        [(fx, "first"), (bx, "second")],
        [(local_tokens, jnp.float32), (local_tokens, jnp.bfloat16)],
    )
    total = keep_far + send(gave, pair).astype(jnp.float32)
    to_back = send(total[:half_rows].astype(wire), back)
    to_ahead = send(total[half_rows:].astype(wire), ahead)
    pad_back = jnp.pad(to_back.astype(jnp.float32), ((0, local_tokens - half_rows), (0, 0)))
    pad_ahead = jnp.pad(to_ahead.astype(jnp.float32), ((half_rows, 0), (0, 0)))
    for r in range(far - 1, 0, -1):
        keep_f, keep_b = keep[r]
        gave = give[r].astype(jnp.float32)
        to_back = send((keep_f + gave[:local_tokens] + pad_back).astype(wire), back)
        to_ahead = send((keep_b + gave[local_tokens:] + pad_ahead).astype(wire), ahead)
        pad_back, pad_ahead = to_back.astype(jnp.float32), to_ahead.astype(jnp.float32)
    total = keep_own + give_own.astype(jnp.float32) + pad_back + pad_ahead
    return total.astype(jnp.bfloat16)


def solution(mesh):
    in_specs = (
        P(("groups", "ep"), None),
        P(("groups", "ep"), None),
        P(("groups", "ep"), None),
        P(("groups", "ep"), None, None),
        P("groups"),
        P("groups"),
    )
    out_specs = P(("groups", "ep"), None)
    return jax.shard_map(shards, mesh=mesh, in_specs=in_specs, out_specs=out_specs, check_vma=False)
```

```python
import functools

import jax
import jax.numpy as jnp
from jax import lax
from jax.experimental import pallas as pl
from jax.experimental.pallas import tpu as pltpu
from jax.sharding import PartitionSpec as P

LANES = 128
SUBS = 16
THIRD = 3
VMEM = pl.BlockSpec(memory_space=pltpu.VMEM)
SMEM = pl.BlockSpec(memory_space=pltpu.SMEM)
HBM = pl.BlockSpec(memory_space=pltpu.HBM)
VMEM_BYTES = 24 * 1024 * 1024


class Packing:
    def __init__(self, local_tokens, feature, experts):
        self.local_tokens = local_tokens
        self.feature = feature
        self.experts = experts
        self.cols = feature // LANES
        self.groups = local_tokens // SUBS
        self.per_tile = max(1, LANES // (2 * experts))
        self.gate_tiles = pl.cdiv(self.groups, self.per_tile)
        self.token_tiles = self.groups * self.cols
        self.tiles = self.token_tiles + self.gate_tiles


def pack_body(pk, capacity, devices, tokens_ref, ids_ref, gates_ref, spare_ref, out_ref):
    for group in range(pk.groups):
        for col in range(pk.cols):
            out_ref[group * pk.cols + col] = tokens_ref[
                group * SUBS : (group + 1) * SUBS, col * LANES : (col + 1) * LANES
            ]
    rows = pk.local_tokens
    lane = lax.broadcasted_iota(jnp.int32, (1, LANES), 1)
    expert = lax.rem(lane, pk.experts)
    ids = ids_ref[...].T
    gates = gates_ref[...].T
    chosen = jnp.zeros((rows, LANES), jnp.float32)
    gate = jnp.zeros((rows, LANES), jnp.float32)
    for k in range(ids.shape[1]):
        match = ids[:, k : k + 1] == expert
        chosen = jnp.where(match, 1.0, chosen)
        gate = jnp.where(match, gates[:, k : k + 1], gate)
    before = (
        lax.broadcasted_iota(jnp.int32, (rows, rows), 0)
        > lax.broadcasted_iota(jnp.int32, (rows, rows), 1)
    ).astype(jnp.float32).astype(jnp.bfloat16)
    arrival = jnp.dot(before, chosen.astype(jnp.bfloat16), preferred_element_type=jnp.float32)
    named = jnp.zeros((1, LANES), jnp.int32)
    for device in range(devices):
        named = named + (expert == spare_ref[device]).astype(jnp.int32)
    count = jnp.ones((1, LANES), jnp.int32)
    for copy in range(1, devices // THIRD + 1):
        count = count + (named >= THIRD * copy).astype(jnp.int32)
    gate = jnp.where(arrival < (count * capacity).astype(jnp.float32), gate, 0.0)
    high = gate.astype(jnp.bfloat16).astype(jnp.float32)
    low = gate - high
    value = jnp.where(lax.rem(lane // pk.experts, 2) == 0, high, low)
    slot = lane // (2 * pk.experts)
    for index in range(pk.gate_tiles):
        tile = jnp.zeros((SUBS, LANES), jnp.float32)
        for part in range(pk.per_tile):
            group = index * pk.per_tile + part
            if group < pk.groups:
                tile = jnp.where(slot == part, value[group * SUBS : (group + 1) * SUBS], tile)
        out_ref[pk.token_tiles + index] = tile.astype(jnp.bfloat16)


def pack(pk, capacity, devices, tokens, ids, gates, spare):
    return pl.pallas_call(
        functools.partial(pack_body, pk, capacity, devices),
        out_shape=jax.ShapeDtypeStruct((pk.tiles, SUBS, LANES), jnp.bfloat16),
        in_specs=[VMEM, VMEM, VMEM, SMEM],
        out_specs=VMEM,
        compiler_params=pltpu.CompilerParams(vmem_limit_bytes=VMEM_BYTES),
        name="pack",
    )(tokens, ids.T, gates.T, spare)


def gather_rows(pk, buffers, x_ref):
    for index, buffer in enumerate(buffers):
        for group in range(pk.groups):
            row = index * pk.local_tokens + group * SUBS
            for col in range(pk.cols):
                x_ref[row : row + SUBS, col * LANES : (col + 1) * LANES] = buffer[
                    group * pk.cols + col
                ]


def activate(gate, up):
    return (gate / (1.0 + jnp.exp(-gate)) * up).astype(jnp.bfloat16)


def down(hidden, weight):
    return lax.dot_general(
        hidden, weight, (((1,), (1,)), ((), ())), preferred_element_type=jnp.float32
    )


def store_scaled(pk, home_ref, me_ref, buffers, answers, out_refs):
    mine = jnp.int32(0)
    for e in range(pk.experts):
        mine = jnp.where(home_ref[e] == me_ref[0], e, mine)
    lane = lax.broadcasted_iota(jnp.int32, (1, LANES), 1)
    scales = []
    for buffer in buffers:
        for group in range(pk.groups):
            place = (group % pk.per_tile) * 2 * pk.experts + mine
            wanted = (lane == place) | (lane == place + pk.experts)
            table = buffer[pk.token_tiles + group // pk.per_tile].astype(jnp.float32)
            scales.append(jnp.sum(jnp.where(wanted, table, 0.0), axis=1, keepdims=True))
    row = 0
    for out_ref in out_refs:
        for start in range(0, out_ref.shape[0], SUBS):
            scaled = answers[row : row + SUBS, :] * scales[row // SUBS]
            out_ref[start : start + SUBS, :] = scaled.astype(out_ref.dtype)
            row += SUBS


def first_body(pk, width, home_ref, me_ref, own_ref, other_ref, weights_ref, *rest):
    keep_ref, give_ref, kept_ref, x_ref, acc_ref, sems = rest
    block = width // THIRD
    copies = []
    for j in range(THIRD):
        for part in range(THIRD):
            columns = slice(part * width + j * block, part * width + (j + 1) * block)
            copy = pltpu.make_async_copy(
                weights_ref.at[0, :, columns], kept_ref.at[:, columns], sems.at[j, part]
            )
            copy.start()
            copies.append(copy)
    gather_rows(pk, [own_ref, other_ref], x_ref)
    rows = x_ref[...]
    for j in range(THIRD):
        for part in range(THIRD):
            copies[j * THIRD + part].wait()
        gate = jnp.dot(
            rows, kept_ref[:, j * block : (j + 1) * block], preferred_element_type=jnp.float32
        )
        up = jnp.dot(
            rows,
            kept_ref[:, width + j * block : width + (j + 1) * block],
            preferred_element_type=jnp.float32,
        )
        part = down(
            activate(gate, up), kept_ref[:, 2 * width + j * block : 2 * width + (j + 1) * block]
        )
        if j == 0:
            acc_ref[...] = part
        else:
            acc_ref[...] += part
    store_scaled(pk, home_ref, me_ref, [own_ref, other_ref], acc_ref, [keep_ref, give_ref])


def first_chunk(pk, weights, home, me, own, other):
    width = weights.shape[2] // 4
    rows, feature = pk.local_tokens, pk.feature
    return pl.pallas_call(
        functools.partial(first_body, pk, width),
        out_shape=[
            jax.ShapeDtypeStruct((rows, feature), jnp.float32),
            jax.ShapeDtypeStruct((rows, feature), jnp.bfloat16),
            pltpu.VMEM((feature, THIRD * width), jnp.bfloat16),
        ],
        in_specs=[SMEM, SMEM, VMEM, VMEM, HBM],
        out_specs=[VMEM, VMEM, VMEM],
        scratch_shapes=[
            pltpu.VMEM((2 * rows, feature), jnp.bfloat16),
            pltpu.VMEM((2 * rows, feature), jnp.float32),
            pltpu.SemaphoreType.DMA((THIRD, THIRD)),
        ],
        compiler_params=pltpu.CompilerParams(vmem_limit_bytes=VMEM_BYTES),
        cost_estimate=pl.CostEstimate(
            flops=4 * rows * feature * 3 * width,
            transcendentals=2 * rows * width,
            bytes_accessed=2 * feature * 3 * width,
        ),
        name="first_chunk",
    )(home, me, own, other, pltpu.with_memory_space_constraint(weights, pltpu.HBM))


def chunk_body(pk, width, count, *refs):
    home_ref, me_ref = refs[:2]
    buffers = refs[2 : 2 + count]
    weights_ref = refs[2 + count]
    out_refs = refs[3 + count : -1]
    x_ref = refs[-1]
    gather_rows(pk, buffers, x_ref)
    rows = x_ref[...]
    gate = jnp.dot(rows, weights_ref[:, :width], preferred_element_type=jnp.float32)
    up = jnp.dot(rows, weights_ref[:, width : 2 * width], preferred_element_type=jnp.float32)
    answers = down(activate(gate, up), weights_ref[:, 2 * width :])
    store_scaled(pk, home_ref, me_ref, buffers, answers, out_refs)


def chunk(pk, weights, home, me, own, crossed):
    width = weights.shape[1] // THIRD
    rows, feature = pk.local_tokens, pk.feature
    buffers = own + crossed
    total = rows * len(buffers)
    return pl.pallas_call(
        functools.partial(chunk_body, pk, width, len(buffers)),
        out_shape=[jax.ShapeDtypeStruct((rows, feature), jnp.float32) for _ in own]
        + [jax.ShapeDtypeStruct((rows * len(crossed), feature), jnp.bfloat16)],
        in_specs=[SMEM, SMEM] + [VMEM] * (len(buffers) + 1),
        out_specs=[VMEM] * (len(own) + 1),
        scratch_shapes=[pltpu.VMEM((total, feature), jnp.bfloat16)],
        compiler_params=pltpu.CompilerParams(vmem_limit_bytes=VMEM_BYTES),
        cost_estimate=pl.CostEstimate(
            flops=2 * total * feature * 3 * width,
            transcendentals=total * width,
            bytes_accessed=2 * feature * 3 * width,
        ),
        name="chunk",
    )(home, me, *buffers, weights)


def shards(tokens, expert_ids, gate_values, expert_weights, home_slot, spare_expert):
    devices = lax.axis_size("ep")
    local_tokens, feature = tokens.shape
    capacity = local_tokens * expert_ids.shape[1] // devices
    pk = Packing(local_tokens, feature, home_slot.shape[0])
    chips = devices // 2
    far = chips // 2
    ring = list(range(0, chips, 2)) + list(range(chips - 1, 0, -2))

    def near(i, core):
        return 2 * ring[(i + (1 if core == 0 else -1)) % chips]

    seats = [(i, core) for i in range(chips) for core in range(2)]
    straight = [(2 * ring[i] + core, near(i, core) + core) for i, core in seats]
    crossing = [(2 * ring[i] + 1 - core, near(i, core) + core) for i, core in seats]
    straight_back = [(t, s) for s, t in straight]
    crossing_back = [(t, s) for s, t in crossing]
    pair = [(d, d ^ 1) for d in range(devices)]
    wire = jnp.bfloat16 if chips <= 8 else jnp.float32

    def send(x, where):
        return lax.ppermute(x, "ep", where)

    me = lax.axis_index("ep").astype(jnp.int32).reshape(1)
    packed = pack(pk, capacity, devices, tokens, expert_ids, gate_values, spare_expert)

    keep, gave = {}, {}
    a, b = send(packed, straight), send(packed, crossing)
    other = send(packed, pair)
    keep[0], give, weights = first_chunk(
        pk, expert_weights, home_slot, me, packed, other
    )
    gave[0] = send(give, pair)
    for r in range(1, far):
        xa, xb = send(a, pair), send(b, pair)
        keep_a, keep_b, give = chunk(pk, weights, home_slot, me, [a, b], [xa, xb])
        keep[r] = (keep_a, keep_b)
        gave[r] = send(give, pair)
        a = send(a, straight)
        if r + 1 < far:
            b = send(b, straight)
    xa = send(a, pair)
    keep_a, give = chunk(pk, weights, home_slot, me, [a], [xa])
    gave[far] = send(give, pair)

    a = (keep_a + gave[far].astype(jnp.float32)).astype(wire)
    a = send(a, straight_back).astype(jnp.float32)
    b = jnp.zeros((), jnp.float32)
    for r in range(far - 1, 0, -1):
        keep_a, keep_b = keep[r]
        a = (a + keep_a + gave[r][:local_tokens].astype(jnp.float32)).astype(wire)
        b = (b + keep_b + gave[r][local_tokens:].astype(jnp.float32)).astype(wire)
        a = send(a, straight_back).astype(jnp.float32)
        b = send(b, straight_back if r > 1 else crossing_back).astype(jnp.float32)
    total = keep[0] + gave[0].astype(jnp.float32) + a + b
    return total.astype(jnp.bfloat16)


def solution(mesh):
    in_specs = (
        P(("groups", "ep"), None),
        P(("groups", "ep"), None),
        P(("groups", "ep"), None),
        P(("groups", "ep"), None, None),
        P("groups"),
        P("groups"),
    )
    out_specs = P(("groups", "ep"), None)

    return jax.shard_map(shards, mesh=mesh, in_specs=in_specs, out_specs=out_specs, check_vma=False)
```

```python
import functools

import jax
import jax.numpy as jnp
from jax import lax
from jax.experimental import pallas as pl
from jax.experimental.pallas import tpu as pltpu
from jax.sharding import PartitionSpec as P

LANES = 128
SUBS = 16
THIRD = 3
VMEM = pl.BlockSpec(memory_space=pltpu.VMEM)
SMEM = pl.BlockSpec(memory_space=pltpu.SMEM)
HBM = pl.BlockSpec(memory_space=pltpu.HBM)
VMEM_BYTES = 20 * 1024 * 1024


class Packing:
    def __init__(self, local_tokens, feature, experts):
        self.local_tokens = local_tokens
        self.feature = feature
        self.experts = experts
        self.cols = feature // LANES
        self.groups = local_tokens // SUBS
        self.per_tile = max(1, LANES // (2 * experts))
        self.gate_tiles = pl.cdiv(self.groups, self.per_tile)
        self.token_tiles = self.groups * self.cols
        self.tiles = self.token_tiles + self.gate_tiles


def pack_body(pk, capacity, devices, me_ref, *refs):
    sources, (out_ref, mine_ref), scratch, sems = refs[:5], refs[5:7], refs[7:12], refs[12]
    copies = [
        pltpu.make_async_copy(source, target, sems.at[index])
        for index, (source, target) in enumerate(zip(sources, scratch))
    ]
    for copy in copies:
        copy.start()
    for copy in copies:
        copy.wait()
    tokens_ref, ids_ref, gates_ref, home_ref, spare_ref = scratch
    for group in range(pk.groups):
        for col in range(pk.cols):
            out_ref[group * pk.cols + col] = tokens_ref[
                group * SUBS : (group + 1) * SUBS, col * LANES : (col + 1) * LANES
            ]
    rows = pk.local_tokens
    lane = lax.broadcasted_iota(jnp.int32, (1, LANES), 1)
    expert = lax.rem(lane, pk.experts)
    ids = ids_ref[...].T
    gates = gates_ref[...].T
    chosen = jnp.zeros((rows, LANES), jnp.float32)
    gate = jnp.zeros((rows, LANES), jnp.float32)
    for k in range(ids.shape[1]):
        match = ids[:, k : k + 1] == expert
        chosen = jnp.where(match, 1.0, chosen)
        gate = jnp.where(match, gates[:, k : k + 1], gate)
    before = (
        lax.broadcasted_iota(jnp.int32, (rows, rows), 0)
        > lax.broadcasted_iota(jnp.int32, (rows, rows), 1)
    ).astype(jnp.float32).astype(jnp.bfloat16)
    arrival = jnp.dot(before, chosen.astype(jnp.bfloat16), preferred_element_type=jnp.float32)
    named = jnp.zeros((1, LANES), jnp.int32)
    mine = jnp.int32(0)
    for index in range(devices):
        named = named + (expert == spare_ref[index]).astype(jnp.int32)
        mine = jnp.where(home_ref[index] == me_ref[0], index, mine)
    mine_ref[...] = jnp.full(mine_ref.shape, mine, jnp.int32)
    count = jnp.ones((1, LANES), jnp.int32)
    for copy in range(1, devices // THIRD + 1):
        count = count + (named >= THIRD * copy).astype(jnp.int32)
    gate = jnp.where(arrival < (count * capacity).astype(jnp.float32), gate, 0.0)
    high = gate.astype(jnp.bfloat16).astype(jnp.float32)
    low = gate - high
    value = jnp.where(lax.rem(lane // pk.experts, 2) == 0, high, low)
    slot = lane // (2 * pk.experts)
    for index in range(pk.gate_tiles):
        tile = jnp.zeros((SUBS, LANES), jnp.float32)
        for part in range(pk.per_tile):
            group = index * pk.per_tile + part
            if group < pk.groups:
                tile = jnp.where(slot == part, value[group * SUBS : (group + 1) * SUBS], tile)
        out_ref[pk.token_tiles + index] = tile.astype(jnp.bfloat16)


def pack(pk, capacity, devices, me, tokens, ids, gates, home, spare):
    sources = [tokens, ids.T, gates.T, home, spare]
    spaces = [pltpu.VMEM, pltpu.VMEM, pltpu.VMEM, pltpu.SMEM, pltpu.SMEM]
    return pl.pallas_call(
        functools.partial(pack_body, pk, capacity, devices),
        out_shape=[
            jax.ShapeDtypeStruct((pk.tiles, SUBS, LANES), jnp.bfloat16),
            pltpu.VMEM((SUBS, LANES), jnp.int32),
        ],
        in_specs=[SMEM] + [HBM] * len(sources),
        out_specs=[VMEM, VMEM],
        scratch_shapes=[space(x.shape, x.dtype) for space, x in zip(spaces, sources)]
        + [pltpu.SemaphoreType.DMA((len(sources),))],
        compiler_params=pltpu.CompilerParams(vmem_limit_bytes=VMEM_BYTES),
        name="pack",
    )(me, *[pltpu.with_memory_space_constraint(x, pltpu.HBM) for x in sources])


def gather_rows(pk, buffers, x_ref):
    for index, buffer in enumerate(buffers):
        for group in range(pk.groups):
            row = index * pk.local_tokens + group * SUBS
            for col in range(pk.cols):
                x_ref[row : row + SUBS, col * LANES : (col + 1) * LANES] = buffer[
                    group * pk.cols + col
                ]


def activate(gate, up):
    return (gate / (1.0 + jnp.exp(-gate)) * up).astype(jnp.bfloat16)


def down(hidden, weight):
    return lax.dot_general(
        hidden, weight, (((1,), (1,)), ((), ())), preferred_element_type=jnp.float32
    )


def store_scaled(pk, mine_ref, buffers, answers, out_refs):
    lane = lax.broadcasted_iota(jnp.int32, (SUBS, LANES), 1)
    scales = []
    for buffer in buffers:
        for group in range(pk.groups):
            place = (group % pk.per_tile) * 2 * pk.experts + mine_ref[...]
            wanted = (lane == place) | (lane == place + pk.experts)
            table = buffer[pk.token_tiles + group // pk.per_tile].astype(jnp.float32)
            scales.append(jnp.sum(jnp.where(wanted, table, 0.0), axis=1, keepdims=True))
    row = 0
    for out_ref in out_refs:
        for start in range(0, out_ref.shape[0], SUBS):
            scaled = answers[row : row + SUBS, :] * scales[row // SUBS]
            out_ref[start : start + SUBS, :] = scaled.astype(out_ref.dtype)
            row += SUBS


def first_body(pk, width, mine_ref, own_ref, weights_ref, *rest):
    keep_ref, kept_ref, x_ref, acc_ref, sems = rest
    block = width // THIRD
    copies = []
    for j in range(THIRD):
        for part in range(THIRD):
            columns = slice(part * width + j * block, part * width + (j + 1) * block)
            copy = pltpu.make_async_copy(
                weights_ref.at[0, :, columns], kept_ref.at[:, columns], sems.at[j, part]
            )
            copy.start()
            copies.append(copy)
    gather_rows(pk, [own_ref], x_ref)
    rows = x_ref[...]
    for j in range(THIRD):
        for part in range(THIRD):
            copies[j * THIRD + part].wait()
        gate = jnp.dot(
            rows, kept_ref[:, j * block : (j + 1) * block], preferred_element_type=jnp.float32
        )
        up = jnp.dot(
            rows,
            kept_ref[:, width + j * block : width + (j + 1) * block],
            preferred_element_type=jnp.float32,
        )
        part = down(
            activate(gate, up), kept_ref[:, 2 * width + j * block : 2 * width + (j + 1) * block]
        )
        if j == 0:
            acc_ref[...] = part
        else:
            acc_ref[...] += part
    store_scaled(pk, mine_ref, [own_ref], acc_ref, [keep_ref])


def first_chunk(pk, weights, mine, own):
    width = weights.shape[2] // 4
    rows, feature = pk.local_tokens, pk.feature
    return pl.pallas_call(
        functools.partial(first_body, pk, width),
        out_shape=[
            pltpu.VMEM((rows, feature), jnp.float32),
            pltpu.VMEM((feature, THIRD * width), jnp.bfloat16),
        ],
        in_specs=[VMEM, VMEM, HBM],
        out_specs=[VMEM, VMEM],
        scratch_shapes=[
            pltpu.VMEM((rows, feature), jnp.bfloat16),
            pltpu.VMEM((rows, feature), jnp.float32),
            pltpu.SemaphoreType.DMA((THIRD, THIRD)),
        ],
        compiler_params=pltpu.CompilerParams(vmem_limit_bytes=VMEM_BYTES),
        cost_estimate=pl.CostEstimate(
            flops=2 * rows * feature * 3 * width,
            transcendentals=rows * width,
            bytes_accessed=2 * feature * 3 * width,
        ),
        name="first_chunk",
    )(mine, own, pltpu.with_memory_space_constraint(weights, pltpu.HBM))


def chunk_body(pk, width, count, *refs):
    mine_ref = refs[0]
    buffers = refs[1 : 1 + count]
    weights_ref = refs[1 + count]
    out_refs = refs[2 + count : -1]
    x_ref = refs[-1]
    gather_rows(pk, buffers, x_ref)
    rows = x_ref[...]
    gate = jnp.dot(rows, weights_ref[:, :width], preferred_element_type=jnp.float32)
    up = jnp.dot(rows, weights_ref[:, width : 2 * width], preferred_element_type=jnp.float32)
    answers = down(activate(gate, up), weights_ref[:, 2 * width :])
    store_scaled(pk, mine_ref, buffers, answers, out_refs)


def chunk(pk, weights, mine, own, crossed):
    width = weights.shape[1] // THIRD
    rows, feature = pk.local_tokens, pk.feature
    buffers = own + crossed
    total = rows * len(buffers)
    return pl.pallas_call(
        functools.partial(chunk_body, pk, width, len(buffers)),
        out_shape=[jax.ShapeDtypeStruct((rows, feature), jnp.float32) for _ in own]
        + [jax.ShapeDtypeStruct((rows * len(crossed), feature), jnp.bfloat16)],
        in_specs=[VMEM] * (len(buffers) + 2),
        out_specs=[VMEM] * (len(own) + 1),
        scratch_shapes=[pltpu.VMEM((total, feature), jnp.bfloat16)],
        compiler_params=pltpu.CompilerParams(vmem_limit_bytes=VMEM_BYTES),
        cost_estimate=pl.CostEstimate(
            flops=2 * total * feature * 3 * width,
            transcendentals=total * width,
            bytes_accessed=2 * feature * 3 * width,
        ),
        name="chunk",
    )(mine, *buffers, weights)


def add_body(starts, *refs):
    out_ref = refs[-1]
    rows = out_ref.shape[0]
    total = refs[0][starts[0] : starts[0] + rows, :].astype(jnp.float32)
    for ref, start in zip(refs[1:-1], starts[1:]):
        total = total + ref[start : start + rows, :].astype(jnp.float32)
    out_ref[...] = total.astype(out_ref.dtype)


def add(rows, dtype, terms):
    arrays = [array for array, _ in terms]
    return pl.pallas_call(
        functools.partial(add_body, [start for _, start in terms]),
        out_shape=jax.ShapeDtypeStruct((rows, arrays[0].shape[1]), dtype),
        in_specs=[VMEM] * len(arrays),
        out_specs=VMEM,
        compiler_params=pltpu.CompilerParams(vmem_limit_bytes=VMEM_BYTES),
        name="add",
    )(*arrays)


def shards(tokens, expert_ids, gate_values, expert_weights, home_slot, spare_expert):
    devices = lax.axis_size("ep")
    local_tokens, feature = tokens.shape
    capacity = local_tokens * expert_ids.shape[1] // devices
    pk = Packing(local_tokens, feature, home_slot.shape[0])
    chips = devices // 2
    far = chips // 2
    ring = list(range(0, chips, 2)) + list(range(chips - 1, 0, -2))

    def near(i, core):
        return 2 * ring[(i + (1 if core == 0 else -1)) % chips]

    seats = [(i, core) for i in range(chips) for core in range(2)]
    straight = [(2 * ring[i] + core, near(i, core) + core) for i, core in seats]
    crossing = [(2 * ring[i] + 1 - core, near(i, core) + core) for i, core in seats]
    straight_back = [(t, s) for s, t in straight]
    crossing_back = [(t, s) for s, t in crossing]
    pair = [(d, d ^ 1) for d in range(devices)]
    wire = jnp.bfloat16 if chips <= 8 else jnp.float32

    def send(x, where):
        return lax.ppermute(x, "ep", where)

    me = lax.axis_index("ep").astype(jnp.int32).reshape(1)
    packed, mine = pack(
        pk, capacity, devices, me, tokens, expert_ids, gate_values, home_slot, spare_expert
    )

    keep, gave = {}, {}
    a, b = send(packed, straight), send(packed, crossing)
    keep_own, weights = first_chunk(pk, expert_weights, mine, packed)
    other = [send(packed, pair)]
    for r in range(1, far):
        xa, xb = send(a, pair), send(b, pair)
        keep_a, keep_b, give = chunk(pk, weights, mine, [a, b], [xa, xb] + other)
        other = []
        keep[r] = (keep_a, keep_b)
        gave[r] = send(give, pair)
        a = send(a, straight)
        if r + 1 < far:
            b = send(b, straight)
    xa = send(a, pair)
    keep_a, give = chunk(pk, weights, mine, [a], [xa])
    gave[far] = send(give, pair)

    half = local_tokens
    a = add(half, wire, [(keep_a, 0), (gave[far], 0)])
    a, b = [(send(a, straight_back), 0)], []
    for r in range(far - 1, 0, -1):
        keep_a, keep_b = keep[r]
        b = add(half, wire, [(keep_b, 0), (gave[r], half)] + b)
        b = [(send(b, straight_back if r > 1 else crossing_back), 0)]
        a = add(half, wire, [(keep_a, 0), (gave[r], 0)] + a)
        a = [(send(a, straight_back), 0)]
    terms = [(keep_own, 0), (gave[1], 2 * half)] + b + a
    return add(half, jnp.bfloat16, terms)


def solution(mesh):
    in_specs = (
        P(("groups", "ep"), None),
        P(("groups", "ep"), None),
        P(("groups", "ep"), None),
        P(("groups", "ep"), None, None),
        P("groups"),
        P("groups"),
    )
    out_specs = P(("groups", "ep"), None)

    return jax.shard_map(shards, mesh=mesh, in_specs=in_specs, out_specs=out_specs, check_vma=False)
```

```python
import functools

import jax
import jax.numpy as jnp
from jax import lax
from jax.experimental import pallas as pl
from jax.experimental.pallas import tpu as pltpu
from jax.sharding import PartitionSpec as P

LANES = 128
SUBS = 16
THIRD = 3
VMEM = pl.BlockSpec(memory_space=pltpu.VMEM)
SMEM = pl.BlockSpec(memory_space=pltpu.SMEM)
HBM = pl.BlockSpec(memory_space=pltpu.HBM)
VMEM_BYTES = 20 * 1024 * 1024


class Packing:
    def __init__(self, local_tokens, feature, experts):
        self.local_tokens = local_tokens
        self.feature = feature
        self.experts = experts
        self.cols = feature // LANES
        self.groups = local_tokens // SUBS
        self.per_tile = max(1, LANES // (2 * experts))
        self.gate_tiles = pl.cdiv(self.groups, self.per_tile)
        self.half = self.groups // 2
        self.split = self.half * self.cols
        self.tiles = self.groups * self.cols + self.gate_tiles

    def tile(self, group):
        return group * self.cols + (self.gate_tiles if group >= self.half else 0)

    def cut(self, packed, part):
        if part == "first":
            return packed[: self.split + self.gate_tiles]
        return packed[self.split :]

    def pieces(self, part):
        picked = range(self.groups)
        shift = 0
        if part == "first":
            picked = range(self.half)
        elif part == "second":
            picked, shift = range(self.half, self.groups), self.split
        return [
            (self.tile(g) - shift, self.split - shift + g // self.per_tile, g % self.per_tile)
            for g in picked
        ]

    def rows(self, part):
        return SUBS * len(self.pieces(part))


def pack_body(pk, capacity, devices, me_ref, *refs):
    sources, (out_ref, mine_ref), scratch, sems = refs[:5], refs[5:7], refs[7:12], refs[12]
    copies = [
        pltpu.make_async_copy(source, target, sems.at[index])
        for index, (source, target) in enumerate(zip(sources, scratch))
    ]
    for copy in copies:
        copy.start()
    for copy in copies:
        copy.wait()
    tokens_ref, ids_ref, gates_ref, home_ref, spare_ref = scratch
    for group in range(pk.groups):
        for col in range(pk.cols):
            out_ref[pk.tile(group) + col] = tokens_ref[
                group * SUBS : (group + 1) * SUBS, col * LANES : (col + 1) * LANES
            ]
    rows = pk.local_tokens
    lane = lax.broadcasted_iota(jnp.int32, (1, LANES), 1)
    expert = lax.rem(lane, pk.experts)
    ids = ids_ref[...].T
    gates = gates_ref[...].T
    chosen = jnp.zeros((rows, LANES), jnp.float32)
    gate = jnp.zeros((rows, LANES), jnp.float32)
    for k in range(ids.shape[1]):
        match = ids[:, k : k + 1] == expert
        chosen = jnp.where(match, 1.0, chosen)
        gate = jnp.where(match, gates[:, k : k + 1], gate)
    before = (
        lax.broadcasted_iota(jnp.int32, (rows, rows), 0)
        > lax.broadcasted_iota(jnp.int32, (rows, rows), 1)
    ).astype(jnp.float32).astype(jnp.bfloat16)
    arrival = jnp.dot(before, chosen.astype(jnp.bfloat16), preferred_element_type=jnp.float32)
    named = jnp.zeros((1, LANES), jnp.int32)
    mine = jnp.int32(0)
    for index in range(devices):
        named = named + (expert == spare_ref[index]).astype(jnp.int32)
        mine = jnp.where(home_ref[index] == me_ref[0], index, mine)
    mine_ref[...] = jnp.full(mine_ref.shape, mine, jnp.int32)
    count = jnp.ones((1, LANES), jnp.int32)
    for copy in range(1, devices // THIRD + 1):
        count = count + (named >= THIRD * copy).astype(jnp.int32)
    gate = jnp.where(arrival < (count * capacity).astype(jnp.float32), gate, 0.0)
    high = gate.astype(jnp.bfloat16).astype(jnp.float32)
    low = gate - high
    value = jnp.where(lax.rem(lane // pk.experts, 2) == 0, high, low)
    slot = lane // (2 * pk.experts)
    for index in range(pk.gate_tiles):
        tile = jnp.zeros((SUBS, LANES), jnp.float32)
        for part in range(pk.per_tile):
            group = index * pk.per_tile + part
            if group < pk.groups:
                tile = jnp.where(slot == part, value[group * SUBS : (group + 1) * SUBS], tile)
        out_ref[pk.split + index] = tile.astype(jnp.bfloat16)


def pack(pk, capacity, devices, me, tokens, ids, gates, home, spare):
    sources = [tokens, ids.T, gates.T, home, spare]
    spaces = [pltpu.VMEM, pltpu.VMEM, pltpu.VMEM, pltpu.SMEM, pltpu.SMEM]
    return pl.pallas_call(
        functools.partial(pack_body, pk, capacity, devices),
        out_shape=[
            jax.ShapeDtypeStruct((pk.tiles, SUBS, LANES), jnp.bfloat16),
            pltpu.VMEM((SUBS, LANES), jnp.int32),
        ],
        in_specs=[SMEM] + [HBM] * len(sources),
        out_specs=[VMEM, VMEM],
        scratch_shapes=[space(x.shape, x.dtype) for space, x in zip(spaces, sources)]
        + [pltpu.SemaphoreType.DMA((len(sources),))],
        compiler_params=pltpu.CompilerParams(vmem_limit_bytes=VMEM_BYTES),
        name="pack",
    )(me, *[pltpu.with_memory_space_constraint(x, pltpu.HBM) for x in sources])


def gather_rows(pk, buffers, parts, x_ref):
    row = 0
    for buffer, part in zip(buffers, parts):
        for first, _, _ in pk.pieces(part):
            for col in range(pk.cols):
                x_ref[row : row + SUBS, col * LANES : (col + 1) * LANES] = buffer[first + col]
            row += SUBS


def activate(gate, up):
    return (gate / (1.0 + jnp.exp(-gate)) * up).astype(jnp.bfloat16)


def down(hidden, weight):
    return lax.dot_general(
        hidden, weight, (((1,), (1,)), ((), ())), preferred_element_type=jnp.float32
    )


def store_scaled(pk, mine_ref, buffers, parts, answers, out_refs):
    lane = lax.broadcasted_iota(jnp.int32, (SUBS, LANES), 1)
    scales = []
    for buffer, part in zip(buffers, parts):
        for _, gate_tile, slot in pk.pieces(part):
            place = slot * 2 * pk.experts + mine_ref[...]
            wanted = (lane == place) | (lane == place + pk.experts)
            table = buffer[gate_tile].astype(jnp.float32)
            scales.append(jnp.sum(jnp.where(wanted, table, 0.0), axis=1, keepdims=True))
    row = 0
    for out_ref in out_refs:
        for start in range(0, out_ref.shape[0], SUBS):
            scaled = answers[row : row + SUBS, :] * scales[row // SUBS]
            out_ref[start : start + SUBS, :] = scaled.astype(out_ref.dtype)
            row += SUBS


def first_body(pk, width, mine_ref, own_ref, weights_ref, *rest):
    keep_ref, kept_ref, x_ref, acc_ref, sems = rest
    block = width // THIRD
    copies = []
    for j in range(THIRD):
        for part in range(THIRD):
            columns = slice(part * width + j * block, part * width + (j + 1) * block)
            copy = pltpu.make_async_copy(
                weights_ref.at[0, :, columns], kept_ref.at[:, columns], sems.at[j, part]
            )
            copy.start()
            copies.append(copy)
    gather_rows(pk, [own_ref], ["all"], x_ref)
    rows = x_ref[...]
    for j in range(THIRD):
        for part in range(THIRD):
            copies[j * THIRD + part].wait()
        gate = jnp.dot(
            rows, kept_ref[:, j * block : (j + 1) * block], preferred_element_type=jnp.float32
        )
        up = jnp.dot(
            rows,
            kept_ref[:, width + j * block : width + (j + 1) * block],
            preferred_element_type=jnp.float32,
        )
        part = down(
            activate(gate, up), kept_ref[:, 2 * width + j * block : 2 * width + (j + 1) * block]
        )
        if j == 0:
            acc_ref[...] = part
        else:
            acc_ref[...] += part
    store_scaled(pk, mine_ref, [own_ref], ["all"], acc_ref, [keep_ref])


def first_chunk(pk, weights, mine, own):
    width = weights.shape[2] // 4
    rows, feature = pk.local_tokens, pk.feature
    return pl.pallas_call(
        functools.partial(first_body, pk, width),
        out_shape=[
            pltpu.VMEM((rows, feature), jnp.float32),
            pltpu.VMEM((feature, THIRD * width), jnp.bfloat16),
        ],
        in_specs=[VMEM, VMEM, HBM],
        out_specs=[VMEM, VMEM],
        scratch_shapes=[
            pltpu.VMEM((rows, feature), jnp.bfloat16),
            pltpu.VMEM((rows, feature), jnp.float32),
            pltpu.SemaphoreType.DMA((THIRD, THIRD)),
        ],
        compiler_params=pltpu.CompilerParams(vmem_limit_bytes=VMEM_BYTES),
        cost_estimate=pl.CostEstimate(
            flops=2 * rows * feature * 3 * width,
            transcendentals=rows * width,
            bytes_accessed=2 * feature * 3 * width,
        ),
        name="first_chunk",
    )(mine, own, pltpu.with_memory_space_constraint(weights, pltpu.HBM))


def chunk_body(pk, width, parts, *refs):
    mine_ref = refs[0]
    count = len(parts)
    buffers = refs[1 : 1 + count]
    weights_ref = refs[1 + count]
    out_refs = refs[2 + count : -1]
    x_ref = refs[-1]
    gather_rows(pk, buffers, parts, x_ref)
    rows = x_ref[...]
    gate = jnp.dot(rows, weights_ref[:, :width], preferred_element_type=jnp.float32)
    up = jnp.dot(rows, weights_ref[:, width : 2 * width], preferred_element_type=jnp.float32)
    answers = down(activate(gate, up), weights_ref[:, 2 * width :])
    store_scaled(pk, mine_ref, buffers, parts, answers, out_refs)


def chunk(pk, weights, mine, own, crossed):
    width = weights.shape[1] // THIRD
    feature = pk.feature
    buffers = [buffer for buffer, _ in own + crossed]
    parts = [part for _, part in own + crossed]
    given = sum(pk.rows(part) for _, part in crossed)
    total = sum(pk.rows(part) for part in parts)
    return pl.pallas_call(
        functools.partial(chunk_body, pk, width, parts),
        out_shape=[jax.ShapeDtypeStruct((pk.rows(part), feature), jnp.float32) for _, part in own]
        + [jax.ShapeDtypeStruct((given, feature), jnp.bfloat16)],
        in_specs=[VMEM] * (len(buffers) + 2),
        out_specs=[VMEM] * (len(own) + 1),
        scratch_shapes=[pltpu.VMEM((total, feature), jnp.bfloat16)],
        compiler_params=pltpu.CompilerParams(vmem_limit_bytes=VMEM_BYTES),
        cost_estimate=pl.CostEstimate(
            flops=2 * total * feature * 3 * width,
            transcendentals=total * width,
            bytes_accessed=2 * feature * 3 * width,
        ),
        name="chunk",
    )(mine, *buffers, weights)


def add_body(places, *refs):
    out_ref = refs[-1]
    rows = out_ref.shape[0]
    cuts = {0, rows}
    for ref, (there, here) in zip(refs, places):
        cuts |= {here, min(rows, here + ref.shape[0] - there)}
    cuts = sorted(cuts)
    for low, high in zip(cuts, cuts[1:]):
        total = None
        for ref, (there, here) in zip(refs, places):
            if here <= low and high - here + there <= ref.shape[0]:
                start = there + low - here
                term = ref[start : start + high - low, :].astype(jnp.float32)
                total = term if total is None else total + term
        out_ref[low:high, :] = total.astype(out_ref.dtype)


def add(rows, dtype, terms):
    arrays = [array for array, _, _ in terms]
    return pl.pallas_call(
        functools.partial(add_body, [(there, here) for _, there, here in terms]),
        out_shape=jax.ShapeDtypeStruct((rows, arrays[0].shape[1]), dtype),
        in_specs=[VMEM] * len(arrays),
        out_specs=VMEM,
        compiler_params=pltpu.CompilerParams(vmem_limit_bytes=VMEM_BYTES),
        name="add",
    )(*arrays)


def shards(tokens, expert_ids, gate_values, expert_weights, home_slot, spare_expert):
    devices = lax.axis_size("ep")
    local_tokens, feature = tokens.shape
    capacity = local_tokens * expert_ids.shape[1] // devices
    pk = Packing(local_tokens, feature, home_slot.shape[0])
    chips = devices // 2
    far = chips // 2
    ring = list(range(0, chips, 2)) + list(range(chips - 1, 0, -2))

    def near(i, core):
        return 2 * ring[(i + (1 if core == 0 else -1)) % chips]

    seats = [(i, core) for i in range(chips) for core in range(2)]
    straight = [(2 * ring[i] + core, near(i, core) + core) for i, core in seats]
    crossing = [(2 * ring[i] + 1 - core, near(i, core) + core) for i, core in seats]
    straight_back = [(t, s) for s, t in straight]
    crossing_back = [(t, s) for s, t in crossing]
    pair = [(d, d ^ 1) for d in range(devices)]
    wire = jnp.bfloat16 if chips <= 8 else jnp.float32

    def send(x, where):
        return lax.ppermute(x, "ep", where)

    me = lax.axis_index("ep").astype(jnp.int32).reshape(1)
    packed, mine = pack(
        pk, capacity, devices, me, tokens, expert_ids, gate_values, home_slot, spare_expert
    )

    keep, gave = {}, {}
    a, b = send(packed, straight), send(packed, crossing)
    keep_own, weights = first_chunk(pk, expert_weights, mine, packed)
    other = [(send(packed, pair), "all")]
    for r in range(1, far):
        xa, xb = send(a, pair), send(b, pair)
        keep_a, keep_b, give = chunk(
            pk, weights, mine, [(a, "all"), (b, "all")], [(xa, "all"), (xb, "all")] + other
        )
        other = []
        keep[r] = (keep_a, keep_b)
        gave[r] = send(give, pair)
        if r + 1 == far:
            a, b = pk.cut(a, "first"), pk.cut(b, "second")
        a, b = send(a, straight), send(b, straight)
    xa, xb = send(a, pair), send(b, pair)
    keep_a, keep_b, give = chunk(
        pk, weights, mine, [(a, "first"), (b, "second")], [(xa, "first"), (xb, "second")]
    )
    gave[far] = send(give, pair)

    rows = local_tokens
    first, second = pk.rows("first"), pk.rows("second")
    a = add(first, wire, [(keep_a, 0, 0), (gave[far], 0, 0)])
    a = [(send(a, straight_back), 0, 0)]
    b = add(second, wire, [(keep_b, 0, 0), (gave[far], first, 0)])
    b = [(send(b, straight_back), 0, first)]
    for r in range(far - 1, 0, -1):
        keep_a, keep_b = keep[r]
        a = add(rows, wire, [(keep_a, 0, 0), (gave[r], 0, 0)] + a)
        a = [(send(a, straight_back), 0, 0)]
        b = add(rows, wire, [(keep_b, 0, 0), (gave[r], rows, 0)] + b)
        b = [(send(b, straight_back if r > 1 else crossing_back), 0, 0)]
    terms = [(keep_own, 0, 0), (gave[1], 2 * rows, 0)] + a + b
    return add(rows, jnp.bfloat16, terms)


def solution(mesh):
    in_specs = (
        P(("groups", "ep"), None),
        P(("groups", "ep"), None),
        P(("groups", "ep"), None),
        P(("groups", "ep"), None, None),
        P("groups"),
        P("groups"),
    )
    out_specs = P(("groups", "ep"), None)

    return jax.shard_map(shards, mesh=mesh, in_specs=in_specs, out_specs=out_specs, check_vma=False)
```

```python
import functools

import jax
import jax.numpy as jnp
from jax import lax
from jax.experimental import pallas as pl
from jax.experimental.pallas import tpu as pltpu
from jax.sharding import PartitionSpec as P

LANES = 128
SUBS = 16
THIRD = 3
COPIES = 8
VMEM = pl.BlockSpec(memory_space=pltpu.VMEM)
SMEM = pl.BlockSpec(memory_space=pltpu.SMEM)
HBM = pl.BlockSpec(memory_space=pltpu.HBM)
VMEM_BYTES = 20 * 1024 * 1024


class Packing:
    def __init__(self, local_tokens, feature, experts):
        self.local_tokens = local_tokens
        self.feature = feature
        self.experts = experts
        self.cols = feature // LANES
        self.groups = local_tokens // SUBS
        self.per_tile = max(1, LANES // (2 * experts))
        self.gate_tiles = pl.cdiv(self.groups, self.per_tile)
        self.half = self.groups // 2
        self.split = self.half * self.cols
        self.tiles = self.groups * self.cols + self.gate_tiles

    def tile(self, group):
        return group * self.cols + (self.gate_tiles if group >= self.half else 0)

    def cut(self, packed, part):
        if part == "first":
            return packed[: self.split + self.gate_tiles]
        return packed[self.split :]

    def pieces(self, part):
        picked = range(self.groups)
        shift = 0
        if part == "first":
            picked = range(self.half)
        elif part == "second":
            picked, shift = range(self.half, self.groups), self.split
        return [
            (self.tile(g) - shift, self.split - shift + g // self.per_tile, g % self.per_tile)
            for g in picked
        ]

    def rows(self, part):
        return SUBS * len(self.pieces(part))


def pack_body(pk, capacity, devices, me_ref, *refs):
    sources, (out_ref, mine_ref), scratch, sems = refs[:5], refs[5:7], refs[7:12], refs[12]
    copies = [
        pltpu.make_async_copy(source, target, sems.at[index])
        for index, (source, target) in enumerate(zip(sources, scratch))
    ]
    for copy in copies:
        copy.start()
    for copy in copies:
        copy.wait()
    tokens_ref, ids_ref, gates_ref, home_ref, spare_ref = scratch
    for group in range(pk.groups):
        for col in range(pk.cols):
            out_ref[pk.tile(group) + col] = tokens_ref[
                group * SUBS : (group + 1) * SUBS, col * LANES : (col + 1) * LANES
            ]
    rows = pk.local_tokens
    lane = lax.broadcasted_iota(jnp.int32, (1, LANES), 1)
    expert = lax.rem(lane, pk.experts)
    ids = ids_ref[...].T
    gates = gates_ref[...].T
    chosen = jnp.zeros((rows, LANES), jnp.float32)
    gate = jnp.zeros((rows, LANES), jnp.float32)
    for k in range(ids.shape[1]):
        match = ids[:, k : k + 1] == expert
        chosen = jnp.where(match, 1.0, chosen)
        gate = jnp.where(match, gates[:, k : k + 1], gate)
    before = (
        lax.broadcasted_iota(jnp.int32, (rows, rows), 0)
        > lax.broadcasted_iota(jnp.int32, (rows, rows), 1)
    ).astype(jnp.float32).astype(jnp.bfloat16)
    arrival = jnp.dot(before, chosen.astype(jnp.bfloat16), preferred_element_type=jnp.float32)
    named = jnp.zeros((1, LANES), jnp.int32)
    mine = jnp.int32(0)
    for index in range(devices):
        named = named + (expert == spare_ref[index]).astype(jnp.int32)
        mine = jnp.where(home_ref[index] == me_ref[0], index, mine)
    mine_ref[...] = jnp.full(mine_ref.shape, mine, jnp.int32)
    count = jnp.ones((1, LANES), jnp.int32)
    for copy in range(1, devices // THIRD + 1):
        count = count + (named >= THIRD * copy).astype(jnp.int32)
    gate = jnp.where(arrival < (count * capacity).astype(jnp.float32), gate, 0.0)
    high = gate.astype(jnp.bfloat16).astype(jnp.float32)
    low = gate - high
    value = jnp.where(lax.rem(lane // pk.experts, 2) == 0, high, low)
    slot = lane // (2 * pk.experts)
    for index in range(pk.gate_tiles):
        tile = jnp.zeros((SUBS, LANES), jnp.float32)
        for part in range(pk.per_tile):
            group = index * pk.per_tile + part
            if group < pk.groups:
                tile = jnp.where(slot == part, value[group * SUBS : (group + 1) * SUBS], tile)
        out_ref[pk.split + index] = tile.astype(jnp.bfloat16)


def pack(pk, capacity, devices, me, tokens, ids, gates, home, spare):
    sources = [tokens, ids.T, gates.T, home, spare]
    spaces = [pltpu.VMEM, pltpu.VMEM, pltpu.VMEM, pltpu.SMEM, pltpu.SMEM]
    return pl.pallas_call(
        functools.partial(pack_body, pk, capacity, devices),
        out_shape=[
            jax.ShapeDtypeStruct((pk.tiles, SUBS, LANES), jnp.bfloat16),
            pltpu.VMEM((SUBS, LANES), jnp.int32),
        ],
        in_specs=[SMEM] + [HBM] * len(sources),
        out_specs=[VMEM, VMEM],
        scratch_shapes=[space(x.shape, x.dtype) for space, x in zip(spaces, sources)]
        + [pltpu.SemaphoreType.DMA((len(sources),))],
        compiler_params=pltpu.CompilerParams(vmem_limit_bytes=VMEM_BYTES),
        name="pack",
    )(me, *[pltpu.with_memory_space_constraint(x, pltpu.HBM) for x in sources])


def gather_rows(pk, buffers, parts, x_ref):
    row = 0
    for buffer, part in zip(buffers, parts):
        for first, _, _ in pk.pieces(part):
            for col in range(pk.cols):
                x_ref[row : row + SUBS, col * LANES : (col + 1) * LANES] = buffer[first + col]
            row += SUBS


def activate(gate, up):
    return (gate / (1.0 + jnp.exp(-gate)) * up).astype(jnp.bfloat16)


def down(hidden, weight):
    return lax.dot_general(
        hidden, weight, (((1,), (1,)), ((), ())), preferred_element_type=jnp.float32
    )


def store_scaled(pk, mine_ref, buffers, parts, answers, out_refs):
    lane = lax.broadcasted_iota(jnp.int32, (SUBS, LANES), 1)
    scales = []
    for buffer, part in zip(buffers, parts):
        for _, gate_tile, slot in pk.pieces(part):
            place = slot * 2 * pk.experts + mine_ref[...]
            wanted = (lane == place) | (lane == place + pk.experts)
            table = buffer[gate_tile].astype(jnp.float32)
            scales.append(jnp.sum(jnp.where(wanted, table, 0.0), axis=1, keepdims=True))
    row = 0
    for out_ref in out_refs:
        for start in range(0, out_ref.shape[0], SUBS):
            scaled = answers[row : row + SUBS, :] * scales[row // SUBS]
            out_ref[start : start + SUBS, :] = scaled.astype(out_ref.dtype)
            row += SUBS


def copy_rows(source_ref, columns, target_ref, sems):
    blocks = sems.shape[0]
    rows = target_ref.shape[0] // blocks
    copies = []
    for index in range(blocks):
        span = slice(index * rows, (index + 1) * rows)
        copy = pltpu.make_async_copy(
            source_ref.at[0, span, columns], target_ref.at[span, :], sems.at[index]
        )
        copy.start()
        copies.append(copy)
    return copies


def fetch_body(columns, weights_ref, kept_ref, sems):
    for copy in copy_rows(weights_ref, columns, kept_ref, sems):
        copy.wait()


def fetch(weights, columns):
    count = columns.stop - columns.start
    return pl.pallas_call(
        functools.partial(fetch_body, columns),
        out_shape=pltpu.VMEM((weights.shape[1], count), weights.dtype),
        in_specs=[HBM],
        out_specs=VMEM,
        scratch_shapes=[pltpu.SemaphoreType.DMA((COPIES,))],
        compiler_params=pltpu.CompilerParams(vmem_limit_bytes=VMEM_BYTES),
        cost_estimate=pl.CostEstimate(
            flops=0, transcendentals=0, bytes_accessed=2 * weights.shape[1] * count
        ),
        name="fetch",
    )(pltpu.with_memory_space_constraint(weights, pltpu.HBM))


def expert(rows, gate_up_ref, down_ref):
    width = down_ref.shape[1]
    gate = jnp.dot(rows, gate_up_ref[:, :width], preferred_element_type=jnp.float32)
    up = jnp.dot(rows, gate_up_ref[:, width:], preferred_element_type=jnp.float32)
    return down(activate(gate, up), down_ref[...])


def chunk_body(pk, parts, *refs):
    mine_ref = refs[0]
    count = len(parts)
    buffers = refs[1 : 1 + count]
    gate_up_ref, down_ref = refs[1 + count : 3 + count]
    out_refs = refs[3 + count : -1]
    x_ref = refs[-1]
    gather_rows(pk, buffers, parts, x_ref)
    answers = expert(x_ref[...], gate_up_ref, down_ref)
    store_scaled(pk, mine_ref, buffers, parts, answers, out_refs)


def chunk(pk, weights, mine, own, crossed):
    gate_up, down_weights = weights
    width = down_weights.shape[1]
    feature = pk.feature
    buffers = [buffer for buffer, _ in own + crossed]
    parts = [part for _, part in own + crossed]
    given = sum(pk.rows(part) for _, part in crossed)
    total = sum(pk.rows(part) for part in parts)
    return pl.pallas_call(
        functools.partial(chunk_body, pk, parts),
        out_shape=[jax.ShapeDtypeStruct((pk.rows(part), feature), jnp.float32) for _, part in own]
        + [jax.ShapeDtypeStruct((given, feature), jnp.bfloat16)],
        in_specs=[VMEM] * (len(buffers) + 3),
        out_specs=[VMEM] * (len(own) + 1),
        scratch_shapes=[pltpu.VMEM((total, feature), jnp.bfloat16)],
        compiler_params=pltpu.CompilerParams(vmem_limit_bytes=VMEM_BYTES),
        cost_estimate=pl.CostEstimate(
            flops=2 * total * feature * 3 * width,
            transcendentals=total * width,
            bytes_accessed=2 * feature * 3 * width,
        ),
        name="chunk",
    )(mine, *buffers, gate_up, down_weights)


def add_body(places, *refs):
    out_ref = refs[-1]
    rows = out_ref.shape[0]
    cuts = {0, rows}
    for ref, (there, here) in zip(refs, places):
        cuts |= {here, min(rows, here + ref.shape[0] - there)}
    cuts = sorted(cuts)
    for low, high in zip(cuts, cuts[1:]):
        total = None
        for ref, (there, here) in zip(refs, places):
            if here <= low and high - here + there <= ref.shape[0]:
                start = there + low - here
                term = ref[start : start + high - low, :].astype(jnp.float32)
                total = term if total is None else total + term
        out_ref[low:high, :] = total.astype(out_ref.dtype)


def add(rows, dtype, terms):
    arrays = [array for array, _, _ in terms]
    return pl.pallas_call(
        functools.partial(add_body, [(there, here) for _, there, here in terms]),
        out_shape=jax.ShapeDtypeStruct((rows, arrays[0].shape[1]), dtype),
        in_specs=[VMEM] * len(arrays),
        out_specs=VMEM,
        compiler_params=pltpu.CompilerParams(vmem_limit_bytes=VMEM_BYTES),
        name="add",
    )(*arrays)


def shards(tokens, expert_ids, gate_values, expert_weights, home_slot, spare_expert):
    devices = lax.axis_size("ep")
    local_tokens, feature = tokens.shape
    capacity = local_tokens * expert_ids.shape[1] // devices
    pk = Packing(local_tokens, feature, home_slot.shape[0])
    chips = devices // 2
    far = chips // 2
    ring = list(range(0, chips, 2)) + list(range(chips - 1, 0, -2))

    def near(i, core):
        return 2 * ring[(i + (1 if core == 0 else -1)) % chips]

    seats = [(i, core) for i in range(chips) for core in range(2)]
    along = [(2 * ring[i] + core, near(i, core) + core) for i, core in seats]
    against = [(t, s) for s, t in along]
    crossing = [(2 * ring[i] + 1 - core, near(i, core) + core) for i, core in seats]
    crossing_back = [(t, s) for s, t in crossing]
    pair = [(d, d ^ 1) for d in range(devices)]
    wire = jnp.bfloat16 if chips <= 8 else jnp.float32

    def send(x, where):
        return lax.ppermute(x, "ep", where)

    me = lax.axis_index("ep").astype(jnp.int32).reshape(1)
    packed, mine = pack(
        pk, capacity, devices, me, tokens, expert_ids, gate_values, home_slot, spare_expert
    )

    keep, gave = {}, {}
    width = expert_weights.shape[2] // 4
    gate_up = fetch(expert_weights, slice(0, 2 * width))
    weights = (gate_up, fetch(expert_weights, slice(2 * width, 3 * width)))
    a, b = send(packed, along), send(packed, crossing)
    other = send(packed, pair)
    keep_own, give = chunk(pk, weights, mine, [(packed, "all")], [(other, "all")])
    gave[0] = send(give, pair)
    for r in range(1, far):
        xa, xb = send(a, pair), send(b, pair)
        keep_a, keep_b, give = chunk(
            pk, weights, mine, [(a, "all"), (b, "all")], [(xa, "all"), (xb, "all")]
        )
        keep[r] = (keep_a, keep_b)
        gave[r] = send(give, pair)
        a = send(a, along)
        if r + 1 < far:
            b = send(b, along)
    xa = send(a, pair)
    keep_a, give = chunk(pk, weights, mine, [(a, "all")], [(xa, "all")])
    gave[far] = send(give, pair)

    rows = local_tokens
    a = add(rows, wire, [(keep_a, 0, 0), (gave[far], 0, 0)])
    a, b = [(send(a, against), 0, 0)], []
    for r in range(far - 1, 0, -1):
        keep_a, keep_b = keep[r]
        a = add(rows, wire, [(keep_a, 0, 0), (gave[r], 0, 0)] + a)
        a = [(send(a, against), 0, 0)]
        b = add(rows, wire, [(keep_b, 0, 0), (gave[r], rows, 0)] + b)
        b = [(send(b, against if r > 1 else crossing_back), 0, 0)]
    terms = [(keep_own, 0, 0), (gave[0], 0, 0)] + a + b
    return add(rows, jnp.bfloat16, terms)


def solution(mesh):
    in_specs = (
        P(("groups", "ep"), None),
        P(("groups", "ep"), None),
        P(("groups", "ep"), None),
        P(("groups", "ep"), None, None),
        P("groups"),
        P("groups"),
    )
    out_specs = P(("groups", "ep"), None)

    return jax.shard_map(shards, mesh=mesh, in_specs=in_specs, out_specs=out_specs, check_vma=False)
```

```python
import functools

import jax
import jax.numpy as jnp
from jax import lax
from jax.experimental import pallas as pl
from jax.experimental.pallas import tpu as pltpu
from jax.sharding import PartitionSpec as P

LANES = 128
SUBS = 16
THIRD = 3
COPIES = 8
PARTS = 2
VMEM = pl.BlockSpec(memory_space=pltpu.VMEM)
SMEM = pl.BlockSpec(memory_space=pltpu.SMEM)
HBM = pl.BlockSpec(memory_space=pltpu.HBM)
VMEM_BYTES = 20 * 1024 * 1024


class Packing:
    def __init__(self, local_tokens, feature, experts):
        self.local_tokens = local_tokens
        self.feature = feature
        self.experts = experts
        self.cols = feature // LANES
        self.groups = local_tokens // SUBS
        self.per_tile = max(1, LANES // (2 * experts))
        self.gate_tiles = pl.cdiv(self.groups, self.per_tile)
        self.half = self.groups // 2
        self.split = self.half * self.cols
        self.tiles = self.groups * self.cols + self.gate_tiles

    def tile(self, group):
        return group * self.cols + (self.gate_tiles if group >= self.half else 0)

    def cut(self, packed, part):
        if part == "first":
            return packed[: self.split + self.gate_tiles]
        return packed[self.split :]

    def pieces(self, part):
        picked = range(self.groups)
        shift = 0
        if part == "first":
            picked = range(self.half)
        elif part == "second":
            picked, shift = range(self.half, self.groups), self.split
        return [
            (self.tile(g) - shift, self.split - shift + g // self.per_tile, g % self.per_tile)
            for g in picked
        ]

    def rows(self, part):
        return SUBS * len(self.pieces(part))


def pack_body(pk, capacity, devices, me_ref, *refs):
    sources, (out_ref, mine_ref), scratch, sems = refs[:5], refs[5:7], refs[7:12], refs[12]
    copies = [
        pltpu.make_async_copy(source, target, sems.at[index])
        for index, (source, target) in enumerate(zip(sources, scratch))
    ]
    for copy in copies:
        copy.start()
    for copy in copies:
        copy.wait()
    tokens_ref, ids_ref, gates_ref, home_ref, spare_ref = scratch
    for group in range(pk.groups):
        for col in range(pk.cols):
            out_ref[pk.tile(group) + col] = tokens_ref[
                group * SUBS : (group + 1) * SUBS, col * LANES : (col + 1) * LANES
            ]
    rows = pk.local_tokens
    lane = lax.broadcasted_iota(jnp.int32, (1, LANES), 1)
    expert = lax.rem(lane, pk.experts)
    ids = ids_ref[...].T
    gates = gates_ref[...].T
    chosen = jnp.zeros((rows, LANES), jnp.float32)
    gate = jnp.zeros((rows, LANES), jnp.float32)
    for k in range(ids.shape[1]):
        match = ids[:, k : k + 1] == expert
        chosen = jnp.where(match, 1.0, chosen)
        gate = jnp.where(match, gates[:, k : k + 1], gate)
    before = (
        lax.broadcasted_iota(jnp.int32, (rows, rows), 0)
        > lax.broadcasted_iota(jnp.int32, (rows, rows), 1)
    ).astype(jnp.float32).astype(jnp.bfloat16)
    arrival = jnp.dot(before, chosen.astype(jnp.bfloat16), preferred_element_type=jnp.float32)
    named = jnp.zeros((1, LANES), jnp.int32)
    mine = jnp.int32(0)
    for index in range(devices):
        named = named + (expert == spare_ref[index]).astype(jnp.int32)
        mine = jnp.where(home_ref[index] == me_ref[0], index, mine)
    mine_ref[...] = jnp.full(mine_ref.shape, mine, jnp.int32)
    count = jnp.ones((1, LANES), jnp.int32)
    for copy in range(1, devices // THIRD + 1):
        count = count + (named >= THIRD * copy).astype(jnp.int32)
    gate = jnp.where(arrival < (count * capacity).astype(jnp.float32), gate, 0.0)
    high = gate.astype(jnp.bfloat16).astype(jnp.float32)
    low = gate - high
    value = jnp.where(lax.rem(lane // pk.experts, 2) == 0, high, low)
    slot = lane // (2 * pk.experts)
    for index in range(pk.gate_tiles):
        tile = jnp.zeros((SUBS, LANES), jnp.float32)
        for part in range(pk.per_tile):
            group = index * pk.per_tile + part
            if group < pk.groups:
                tile = jnp.where(slot == part, value[group * SUBS : (group + 1) * SUBS], tile)
        out_ref[pk.split + index] = tile.astype(jnp.bfloat16)


def pack(pk, capacity, devices, me, tokens, ids, gates, home, spare):
    sources = [tokens, ids.T, gates.T, home, spare]
    spaces = [pltpu.VMEM, pltpu.VMEM, pltpu.VMEM, pltpu.SMEM, pltpu.SMEM]
    return pl.pallas_call(
        functools.partial(pack_body, pk, capacity, devices),
        out_shape=[
            jax.ShapeDtypeStruct((pk.tiles, SUBS, LANES), jnp.bfloat16),
            pltpu.VMEM((SUBS, LANES), jnp.int32),
        ],
        in_specs=[SMEM] + [HBM] * len(sources),
        out_specs=[VMEM, VMEM],
        scratch_shapes=[space(x.shape, x.dtype) for space, x in zip(spaces, sources)]
        + [pltpu.SemaphoreType.DMA((len(sources),))],
        compiler_params=pltpu.CompilerParams(vmem_limit_bytes=VMEM_BYTES),
        name="pack",
    )(me, *[pltpu.with_memory_space_constraint(x, pltpu.HBM) for x in sources])


def gather_rows(pk, buffers, parts, x_ref):
    row = 0
    for buffer, part in zip(buffers, parts):
        for first, _, _ in pk.pieces(part):
            for col in range(pk.cols):
                x_ref[row : row + SUBS, col * LANES : (col + 1) * LANES] = buffer[first + col]
            row += SUBS


def activate(gate, up):
    return (gate / (1.0 + jnp.exp(-gate)) * up).astype(jnp.bfloat16)


def down(hidden, weight):
    return lax.dot_general(
        hidden, weight, (((1,), (1,)), ((), ())), preferred_element_type=jnp.float32
    )


def store_scaled(pk, mine_ref, buffers, parts, answers, out_refs):
    lane = lax.broadcasted_iota(jnp.int32, (SUBS, LANES), 1)
    scales = []
    for buffer, part in zip(buffers, parts):
        for _, gate_tile, slot in pk.pieces(part):
            place = slot * 2 * pk.experts + mine_ref[...]
            wanted = (lane == place) | (lane == place + pk.experts)
            table = buffer[gate_tile].astype(jnp.float32)
            scales.append(jnp.sum(jnp.where(wanted, table, 0.0), axis=1, keepdims=True))
    row = 0
    for out_ref in out_refs:
        for start in range(0, out_ref.shape[0], SUBS):
            scaled = answers[row : row + SUBS, :] * scales[row // SUBS]
            out_ref[start : start + SUBS, :] = scaled.astype(out_ref.dtype)
            row += SUBS


def copy_rows(source_ref, columns, target_ref, sems):
    blocks = sems.shape[0]
    rows = target_ref.shape[0] // blocks
    copies = []
    for index in range(blocks):
        span = slice(index * rows, (index + 1) * rows)
        copy = pltpu.make_async_copy(
            source_ref.at[0, span, columns], target_ref.at[span, :], sems.at[index]
        )
        copy.start()
        copies.append(copy)
    return copies


def fetch_body(columns, weights_ref, kept_ref, sems):
    for copy in copy_rows(weights_ref, columns, kept_ref, sems):
        copy.wait()


def fetch(weights, columns):
    count = columns.stop - columns.start
    return pl.pallas_call(
        functools.partial(fetch_body, columns),
        out_shape=pltpu.VMEM((weights.shape[1], count), weights.dtype),
        in_specs=[HBM],
        out_specs=VMEM,
        scratch_shapes=[pltpu.SemaphoreType.DMA((COPIES,))],
        compiler_params=pltpu.CompilerParams(vmem_limit_bytes=VMEM_BYTES),
        cost_estimate=pl.CostEstimate(
            flops=0, transcendentals=0, bytes_accessed=2 * weights.shape[1] * count
        ),
        name="fetch",
    )(pltpu.with_memory_space_constraint(weights, pltpu.HBM))


def expert(rows, gate_up_ref, down_ref):
    width = down_ref.shape[1]
    gate = jnp.dot(rows, gate_up_ref[:, :width], preferred_element_type=jnp.float32)
    up = jnp.dot(rows, gate_up_ref[:, width:], preferred_element_type=jnp.float32)
    return down(activate(gate, up), down_ref[...])


def chunk_body(pk, parts, *refs):
    mine_ref = refs[0]
    count = len(parts)
    buffers = refs[1 : 1 + count]
    gate_up_ref, down_ref = refs[1 + count : 3 + count]
    out_refs = refs[3 + count : -1]
    x_ref = refs[-1]
    gather_rows(pk, buffers, parts, x_ref)
    answers = expert(x_ref[...], gate_up_ref, down_ref)
    store_scaled(pk, mine_ref, buffers, parts, answers, out_refs)


def chunk(pk, weights, mine, own, crossed):
    gate_up, down_weights = weights
    width = down_weights.shape[1]
    feature = pk.feature
    buffers = [buffer for buffer, _ in own + crossed]
    parts = [part for _, part in own + crossed]
    given = sum(pk.rows(part) for _, part in crossed)
    total = sum(pk.rows(part) for part in parts)
    return pl.pallas_call(
        functools.partial(chunk_body, pk, parts),
        out_shape=[jax.ShapeDtypeStruct((pk.rows(part), feature), jnp.float32) for _, part in own]
        + [jax.ShapeDtypeStruct((given, feature), jnp.bfloat16)],
        in_specs=[VMEM] * (len(buffers) + 3),
        out_specs=[VMEM] * (len(own) + 1),
        scratch_shapes=[pltpu.VMEM((total, feature), jnp.bfloat16)],
        compiler_params=pltpu.CompilerParams(vmem_limit_bytes=VMEM_BYTES),
        cost_estimate=pl.CostEstimate(
            flops=2 * total * feature * 3 * width,
            transcendentals=total * width,
            bytes_accessed=2 * feature * 3 * width,
        ),
        name="chunk",
    )(mine, *buffers, gate_up, down_weights)


def add_body(places, *refs):
    out_ref = refs[-1]
    rows = out_ref.shape[0]
    cuts = {0, rows}
    for ref, (there, here) in zip(refs, places):
        cuts |= {here, min(rows, here + ref.shape[0] - there)}
    cuts = sorted(cuts)
    for low, high in zip(cuts, cuts[1:]):
        total = None
        for ref, (there, here) in zip(refs, places):
            if here <= low and high - here + there <= ref.shape[0]:
                start = there + low - here
                term = ref[start : start + high - low, :].astype(jnp.float32)
                total = term if total is None else total + term
        out_ref[low:high, :] = total.astype(out_ref.dtype)


def add(rows, dtype, terms):
    arrays = [array for array, _, _ in terms]
    return pl.pallas_call(
        functools.partial(add_body, [(there, here) for _, there, here in terms]),
        out_shape=jax.ShapeDtypeStruct((rows, arrays[0].shape[1]), dtype),
        in_specs=[VMEM] * len(arrays),
        out_specs=VMEM,
        compiler_params=pltpu.CompilerParams(vmem_limit_bytes=VMEM_BYTES),
        name="add",
    )(*arrays)


def shards(tokens, expert_ids, gate_values, expert_weights, home_slot, spare_expert):
    devices = lax.axis_size("ep")
    local_tokens, feature = tokens.shape
    capacity = local_tokens * expert_ids.shape[1] // devices
    pk = Packing(local_tokens, feature, home_slot.shape[0])
    chips = devices // 2
    far = chips // 2
    ring = list(range(0, chips, 2)) + list(range(chips - 1, 0, -2))

    def near(i, core):
        return 2 * ring[(i + (1 if core == 0 else -1)) % chips]

    seats = [(i, core) for i in range(chips) for core in range(2)]
    along = [(2 * ring[i] + core, near(i, core) + core) for i, core in seats]
    against = [(t, s) for s, t in along]
    crossing = [(2 * ring[i] + 1 - core, near(i, core) + core) for i, core in seats]
    crossing_back = [(t, s) for s, t in crossing]
    pair = [(d, d ^ 1) for d in range(devices)]
    wire = jnp.bfloat16 if chips <= 8 else jnp.float32

    def send(x, where):
        return lax.ppermute(x, "ep", where)

    me = lax.axis_index("ep").astype(jnp.int32).reshape(1)
    packed, mine = pack(
        pk, capacity, devices, me, tokens, expert_ids, gate_values, home_slot, spare_expert
    )

    keep, gave = {}, {}
    width = expert_weights.shape[2] // 4
    gate_up = fetch(expert_weights, slice(0, 2 * width))
    weights = (gate_up, fetch(expert_weights, slice(2 * width, 3 * width)))
    a, b = send(packed, along), send(packed, crossing)
    other = send(packed, pair)
    keep_own, give = chunk(pk, weights, mine, [(packed, "all")], [(other, "all")])
    gave[0] = send(give, pair)
    for r in range(1, far):
        xa, xb = send(a, pair), send(b, pair)
        keep_a, keep_b, give = chunk(
            pk, weights, mine, [(a, "all"), (b, "all")], [(xa, "all"), (xb, "all")]
        )
        keep[r] = (keep_a, keep_b)
        gave[r] = send(give, pair)
        a = send(a, along)
        if r + 1 < far:
            b = send(b, along)
    xa = send(a, pair)
    keep_a, give = chunk(pk, weights, mine, [(a, "all")], [(xa, "all")])
    gave[far] = send(give, pair)

    rows = local_tokens
    size = rows // PARTS
    keep[far] = (keep_a, None)
    sent = {"a": [[]] * PARTS, "b": [[]] * PARTS}
    for r in range(far, 0, -1):
        for chain, kept, first in (("a", keep[r][0], 0), ("b", keep[r][1], rows)):
            if kept is None:
                continue
            route = crossing_back if chain == "b" and r == 1 else against
            earlier, sent[chain] = sent[chain], []
            for part in range(PARTS):
                at = part * size
                terms = [(kept, at, 0), (gave[r], first + at, 0)] + earlier[part]
                total = add(size, wire, terms)
                sent[chain].append([(send(total, route), 0, 0)])
    terms = [(keep_own, 0, 0), (gave[0], 0, 0)]
    for chain in sent.values():
        terms += [(array, 0, part * size) for part, [(array, _, _)] in enumerate(chain)]
    return add(rows, jnp.bfloat16, terms)


def solution(mesh):
    in_specs = (
        P(("groups", "ep"), None),
        P(("groups", "ep"), None),
        P(("groups", "ep"), None),
        P(("groups", "ep"), None, None),
        P("groups"),
        P("groups"),
    )
    out_specs = P(("groups", "ep"), None)

    return jax.shard_map(shards, mesh=mesh, in_specs=in_specs, out_specs=out_specs, check_vma=False)
```
